32 devices in a mesh: user: 8 (over z, x), item: 4 (over y, core).
Axes of the slice: x: 2, y: 2, z: 4, core: 2. Of those that a mesh axis runs over, the one named last changes fastest.
Arguments:
- ratings: bfloat16 [32768, 8192], P('user', 'item'), may hold values from -6 to 6
- tile_mask: int32 [128, 32], P('user', 'item'), may hold values 0 or 1
- user_factors: bfloat16 [128, 256, 128], P('user', 'item'), may hold values from -1.796875 to 1.796875
- item_factors: bfloat16 [8192, 128], P('item'), may hold values from -1.796875 to 1.796875
- neighbours: int32 [128, 4], replicated, may hold values from 0 to 127, as said below
- edge_weight: float32 [128, 4], replicated, may hold values from 0.5 to 8
- dual: float32 [128, 4, 256, 128], P('user', None, 'item'), may hold values from -1.8 to 1.8
Outputs:
- user_update: float32 [128, 256, 128], P('user', 'item')
- dual_update: float32 [128, 4, 256, 128], P('user', None, 'item')
- item_gradient: float32 [8192, 128], P('item')
The draws below stay inside these ranges and needn't reach their ends.
Inputs may be any that keep to these rules, and one draw needn't show every extreme that they name: `neighbours`: among the 64 entries of rows d * 16 to (d + 1) * 16 - 1, for any d, at most 16 name blocks of one group c * 16 to (c + 1) * 16 - 1, and some group is named exactly 16 times.
All inputs are finite; a program needn't handle non-finite values. No bound on the sum of `tile_mask` on one device may be relied on, other than what follows from the above.
Results may differ from the reference program's by a relative error of at most 0.0012.
Values may be sent and summed in bfloat16 or wider, within the bound.
A program may use at most 128 MiB of HBM per device.

```python
import math
import jax
import jax.numpy as jnp
from jax import lax

R = 128
BROWS = 256
K = 4
ITILE = 256
ITERS = 2
BLK_DEV = 16
BLOCKS = 128
USERS = 32768
ITEMS = 8192
CAP = 16
N_USER = 8


def draw_neighbours(key, part):
    edges_per = BLK_DEV * K

    def one_device(device_key):
        key_main, key_rest, key_order, key_block = jax.random.split(device_key, 4)
        main_owner = jax.random.randint(key_main, (), 0, N_USER)
        spread = (main_owner + 1 + jnp.arange((N_USER - 1) * CAP) // CAP) % N_USER
        spread = jax.random.permutation(key_rest, spread)[:edges_per - CAP]
        owners = jnp.concatenate([jnp.full((CAP,), main_owner, jnp.int32), spread.astype(jnp.int32)])
        owners = jax.random.permutation(key_order, owners)
        within = jax.random.randint(key_block, (edges_per,), 0, BLK_DEV)
        return (owners * BLK_DEV + within).astype(jnp.int32)
    device_keys = jax.random.split(jax.random.fold_in(key, 7), N_USER)
    return jax.vmap(one_device)(device_keys).reshape(BLOCKS, K)


def set_ends(result, key, least, high):
    index_at = [jax.random.randint(jax.random.fold_in(key, axis), (), 0, length) for axis, length in enumerate(result.shape)]
    widest = result.shape.index(max(result.shape))
    beside = index_at[:widest] + [(index_at[widest] + 1) % result.shape[widest]] + index_at[widest + 1:]
    return result.at[tuple(index_at)].set(least).at[tuple(beside)].set(high)


def level_of(own_key, extent, shards, low, high):
    loudness = 1.0
    for dim, parts in shards:
        steps = jax.random.uniform(jax.random.fold_in(jax.random.fold_in(own_key, 6), dim), (parts,), jnp.float32, low / len(shards), high / len(shards))
        loudness = loudness * jnp.repeat(jnp.exp(steps), extent[dim] // parts).reshape((-1,) + (1,) * (len(extent) - 1 - dim))
    return loudness


def noise(stream_key, dims, deviation, limit, pieces=(), kind=jnp.bfloat16):
    factor_of = level_of(stream_key, dims, pieces, -0.22, 0.18) if pieces else 1.0
    drawn = jax.random.normal(stream_key, dims, jnp.float32) * deviation * factor_of
    return jnp.minimum(jnp.maximum(drawn, -limit), limit).astype(kind)


def setup_inputs(seed: int = 0) -> dict:
    keys = jax.random.split(jax.random.key(seed), 8)
    ratings = noise(keys[0], (USERS, ITEMS), 1.0, 6.0, ((0, 8), (1, 4)))
    tile_mask = set_ends((jax.random.randint(keys[1], (BLOCKS, ITEMS // ITILE), 0, 2) < 1).astype(jnp.int32), jax.random.fold_in(keys[1], 1), 0, 1)
    user_factors = noise(keys[2], (BLOCKS, BROWS, R), 0.3, 1.796875, ((0, 8), (1, 4)))
    item_factors = noise(keys[3], (ITEMS, R), 0.3, 1.796875, ((0, 4),))
    neighbours = draw_neighbours(jax.random.fold_in(keys[7], 71), 0)
    edge_weight = jnp.clip(jnp.exp(jax.random.uniform(keys[5], (BLOCKS, K), jnp.float32, math.log(0.5), math.log(8.0))), 0.5, 8.0)
    dual = noise(keys[6], (BLOCKS, K, BROWS, R), 0.3, 1.8, ((0, 8), (2, 4)), jnp.float32)
    return dict(ratings=ratings, tile_mask=tile_mask, user_factors=user_factors, item_factors=item_factors, neighbours=neighbours, edge_weight=edge_weight, dual=dual)


descent = 0.5
dual_step = 0.5
primal_step = 0.25

def reference(ratings, tile_mask, user_factors, item_factors, neighbours, edge_weight, dual):
    rating_blocks = ratings.reshape(BLOCKS, BROWS, ITEMS)

    def one_block(carry, inputs):
        users_block, rating_block, tile_row = inputs
        scores = jnp.dot(users_block, item_factors.T, preferred_element_type=jnp.float32)
        observed = jnp.repeat(tile_row.astype(jnp.float32), ITILE)[None, :]
        errors = (observed * (scores - rating_block.astype(jnp.float32))).astype(jnp.bfloat16)
        user_term = jnp.dot(errors, item_factors, preferred_element_type=jnp.float32)
        item_term = jnp.dot(errors.T, users_block, preferred_element_type=jnp.float32)
        return (carry + item_term, user_term)
    item_part, user_part = lax.scan(one_block, jnp.zeros((ITEMS, R), jnp.float32), (user_factors, rating_blocks, tile_mask))
    item_gradient = item_part / math.sqrt(USERS)
    user_grad = user_part / math.sqrt(ITEMS)
    target = user_factors.astype(jnp.float32) - descent * user_grad
    targets_flat = neighbours.reshape(-1).astype(jnp.int32)
    radius = edge_weight.reshape(-1)[:, None]
    primal = target
    extra = target
    flux = dual.reshape(BLOCKS * K, BROWS, R)
    for sweep in range(ITERS):
        moved = flux + dual_step * (jnp.repeat(extra, K, axis=0) - extra[targets_flat])
        length = jnp.sqrt(lax.optimization_barrier(jnp.sum(moved * moved, axis=-1)))
        flux = moved * (radius / jnp.maximum(length, radius))[..., None]
        inflow = jax.ops.segment_sum(flux, targets_flat, num_segments=BLOCKS)
        divergence = lax.optimization_barrier(jnp.sum(flux.reshape(BLOCKS, K, BROWS, R), axis=1)) - inflow
        newer = (primal - primal_step * divergence + primal_step * target) / (1.0 + primal_step)
        extra = 2.0 * newer - primal
        primal = newer
    return (primal, flux.reshape(BLOCKS, K, BROWS, R), item_gradient)
```

```python
import functools
import math

import jax
import jax.numpy as jnp
from jax import lax
from jax.experimental import pallas as pl
from jax.experimental.pallas import tpu as pltpu
from jax.sharding import PartitionSpec as P

ITERS = 2

descent = 0.5
dual_step = 0.5
primal_step = 0.25


def gradient_kernel(tiles, mask_ref, piece_ref, rating_ref, item_ref, user_out, item_out):
    b = pl.program_id(0)
    width = item_ref.shape[0] // tiles

    @pl.when(b == 0)
    def _():
        item_out[...] = jnp.zeros_like(item_out)

    user_out[...] = jnp.zeros_like(user_out)
    for t in range(tiles):

        @pl.when(mask_ref[b, t] != 0)
        def _():
            cols = pl.ds(t * width, width)
            users = piece_ref[0]
            items = item_ref[cols, :]
            scores = lax.dot_general(
                users, items, (((1,), (1,)), ((), ())), preferred_element_type=jnp.float32
            )
            errors = (scores - rating_ref[:, cols].astype(jnp.float32)).astype(jnp.bfloat16)
            user_out[0] += jnp.dot(errors, items, preferred_element_type=jnp.float32)
            item_out[cols, :] += lax.dot_general(
                errors, users, (((0,), (0,)), ((), ())), preferred_element_type=jnp.float32
            )


def gradients(tile_mask, piece, ratings, item_factors):
    blocks, rows, width = piece.shape
    cols = item_factors.shape[0]
    tiles = tile_mask.shape[1]
    return pl.pallas_call(
        functools.partial(gradient_kernel, tiles),
        out_shape=(
            jax.ShapeDtypeStruct((blocks, rows, width), jnp.float32),
            jax.ShapeDtypeStruct((cols, width), jnp.float32),
        ),
        grid_spec=pltpu.PrefetchScalarGridSpec(
            num_scalar_prefetch=1,
            grid=(blocks,),
            in_specs=[
                pl.BlockSpec((1, rows, width), lambda b, m: (b, 0, 0)),
                pl.BlockSpec((rows, cols), lambda b, m: (b, 0)),
                pl.BlockSpec((cols, width), lambda b, m: (0, 0)),
            ],
            out_specs=[
                pl.BlockSpec((1, rows, width), lambda b, m: (b, 0, 0)),
                pl.BlockSpec((cols, width), lambda b, m: (0, 0)),
            ],
        ),
        compiler_params=pltpu.CompilerParams(vmem_limit_bytes=32 << 20),
        cost_estimate=pl.CostEstimate(
            flops=6 * blocks * rows * cols * width,
            bytes_accessed=2 * blocks * rows * cols,
            transcendentals=0,
        ),
    )(tile_mask, piece, ratings, item_factors)


def variation_kernel(group, near_ref, weight_ref, target_ref, dual_ref, out_ref, extra_ref, div_ref):
    blocks, degree = dual_ref.shape[:2]

    for sweep in range(ITERS):
        source = target_ref if sweep == 0 else extra_ref
        div_ref[...] = jnp.zeros_like(div_ref)

        def edges(step, _):
            first = step * group
            todo = []
            for j in range(group):
                a = first + j
                here = source[a]
                total = None
                for k in range(degree):
                    e = a * degree + k
                    to = near_ref[e]
                    w = weight_ref[e]
                    flux = dual_ref[a, k] if sweep == 0 else out_ref[a, k]
                    moved = flux + dual_step * (here - source[to])
                    square = jnp.sum(moved * moved, axis=-1, keepdims=True)
                    flux = moved * (w * lax.rsqrt(jnp.maximum(square, w * w)))
                    out_ref[a, k] = flux
                    total = flux if total is None else total + flux
                    todo.append((to, -flux))
                todo.append((a, total))
            for place, term in todo:
                div_ref[place] += term
            return 0

        lax.fori_loop(0, blocks // group, edges, 0)

        target = target_ref[...]
        primal = target if sweep == 0 else out_ref[:, degree]
        newer = (primal - primal_step * div_ref[...] + primal_step * target) / (1.0 + primal_step)
        if sweep < ITERS - 1:
            extra_ref[...] = 2.0 * newer - primal
        out_ref[:, degree] = newer


def variation(near, weight, target, dual):
    blocks, degree, rows, width = dual.shape
    group = next(g for g in (4, 2, 1) if blocks % g == 0)
    vmem = pl.BlockSpec(memory_space=pltpu.VMEM)
    smem = pl.BlockSpec(memory_space=pltpu.SMEM)
    return pl.pallas_call(
        functools.partial(variation_kernel, group),
        out_shape=jax.ShapeDtypeStruct((blocks, degree + 1, rows, width), jnp.float32),
        in_specs=[smem, smem, vmem, vmem],
        out_specs=vmem,
        scratch_shapes=[
            pltpu.VMEM((blocks, rows, width), jnp.float32),
            pltpu.VMEM((blocks, rows, width), jnp.float32),
        ],
        compiler_params=pltpu.CompilerParams(vmem_limit_bytes=32 << 20),
        cost_estimate=pl.CostEstimate(
            flops=20 * ITERS * dual.size, bytes_accessed=8 * dual.size, transcendentals=0
        ),
    )(near.reshape(-1), weight.reshape(-1), target, dual)


def shards(ratings, tile_mask, user_factors, item_factors, neighbours, edge_weight, dual):
    blocks_here, sub_rows, width = user_factors.shape
    degree = neighbours.shape[1]
    user_count = lax.axis_size("user")
    item_count = lax.axis_size("item")
    item_cols = item_factors.shape[0]
    thin = sub_rows // user_count
    total_blocks = blocks_here * user_count

    dual_parts = dual.reshape(blocks_here, degree, user_count, thin, width).transpose(2, 0, 1, 3, 4)
    dual_rows = lax.all_to_all(dual_parts, "user", 0, 0, tiled=True).reshape(
        total_blocks, degree, thin, width
    )

    piece = lax.all_gather(user_factors, "item", axis=1, tiled=True)
    user_term, item_term = gradients(tile_mask, piece, ratings, item_factors)
    total_users = blocks_here * sub_rows * item_count * user_count
    total_items = item_cols * item_count
    user_grad = lax.psum_scatter(user_term, "item", scatter_dimension=1, tiled=True) / math.sqrt(
        total_items
    )
    item_grad = lax.psum(item_term, "user") / math.sqrt(total_users)
    target = user_factors.astype(jnp.float32) - descent * user_grad
    target_parts = target.reshape(blocks_here, user_count, thin, width).transpose(1, 0, 2, 3)
    target_rows = lax.all_to_all(target_parts, "user", 0, 0, tiled=True).reshape(
        total_blocks, thin, width
    )
    result = variation(neighbours, edge_weight, target_rows, dual_rows)
    result = result.reshape(user_count, blocks_here, degree + 1, thin, width)
    result = lax.all_to_all(result, "user", 0, 0, tiled=True)
    result = result.transpose(1, 2, 0, 3, 4).reshape(blocks_here, degree + 1, sub_rows, width)
    return (result[:, degree], result[:, :degree], item_grad)


def solution(mesh):
    in_specs = (
        P("user", "item"),
        P("user", "item"),
        P("user", "item", None),
        P("item", None),
        P(),
        P(),
        P("user", None, "item", None),
    )
    out_specs = (P("user", "item", None), P("user", None, "item", None), P("item", None))
    return jax.shard_map(shards, mesh=mesh, in_specs=in_specs, out_specs=out_specs, check_vma=False)
```

```python
import functools
import math

import jax
import jax.numpy as jnp
from jax import lax
from jax.experimental import pallas as pl
from jax.experimental.pallas import tpu as pltpu
from jax.sharding import PartitionSpec as P

ITERS = 2
PAIR = 2
WIRE = jnp.float16

descent = 0.5
dual_step = 0.5
primal_step = 0.25


def gradient_kernel(tiles, mask_ref, piece_ref, rating_ref, item_ref, user_out, item_out, active, total):
    b = pl.program_id(0)
    width = item_ref.shape[0] // tiles
    parts, _, sub, rank = user_out.shape

    @pl.when(b == 0)
    def _():
        total[...] = jnp.zeros_like(total)

    count = 0
    for t in range(tiles):
        active[count] = t
        count = count + jnp.where(mask_ref[b, t] != 0, 1, 0)

    user_out[...] = jnp.zeros_like(user_out)
    users = piece_ref[0]
    across = users.T

    def pair(step, _):
        first = step * PAIR
        user_sum = None
        for j in range(PAIR):
            at = jnp.minimum(first + j, count - 1)
            keep = jnp.where(first + j < count, 1.0, 0.0)
            cols = pl.ds(pl.multiple_of(active[at] * width, width), width)
            items = item_ref[cols, :]
            scores = lax.dot_general(
                users, items, (((1,), (1,)), ((), ())), preferred_element_type=jnp.float32
            )
            errors = (keep * (scores - rating_ref[:, cols].astype(jnp.float32))).astype(jnp.bfloat16)
            term = jnp.dot(errors, items, preferred_element_type=jnp.float32)
            user_sum = term if user_sum is None else user_sum + term
            total[:, cols] += jnp.dot(across, errors, preferred_element_type=jnp.float32)
        for p in range(parts):
            user_out[p, 0] += user_sum[p * sub : (p + 1) * sub]
        return 0

    lax.fori_loop(0, (count + PAIR - 1) // PAIR, pair, 0)

    @pl.when(b == pl.num_programs(0) - 1)
    def _():
        item_out[...] = total[...].T


def gradients(tile_mask, piece, ratings, item_factors, parts):
    blocks, rows, width = piece.shape
    cols = item_factors.shape[0]
    tiles = tile_mask.shape[1]
    sub = rows // parts
    return pl.pallas_call(
        functools.partial(gradient_kernel, tiles),
        out_shape=(
            jax.ShapeDtypeStruct((parts, blocks, sub, width), jnp.float32),
            jax.ShapeDtypeStruct((cols, width), jnp.float32),
        ),
        grid_spec=pltpu.PrefetchScalarGridSpec(
            num_scalar_prefetch=1,
            grid=(blocks,),
            in_specs=[
                pl.BlockSpec((1, rows, width), lambda b, m: (b, 0, 0)),
                pl.BlockSpec((rows, cols), lambda b, m: (b, 0)),
                pl.BlockSpec((cols, width), lambda b, m: (0, 0)),
            ],
            out_specs=[
                pl.BlockSpec((parts, 1, sub, width), lambda b, m: (0, b, 0, 0)),
                pl.BlockSpec((cols, width), lambda b, m: (0, 0)),
            ],
            scratch_shapes=[
                pltpu.SMEM((tiles + 1,), jnp.int32),
                pltpu.VMEM((width, cols), jnp.float32),
            ],
        ),
        compiler_params=pltpu.CompilerParams(vmem_limit_bytes=52 << 20),
        cost_estimate=pl.CostEstimate(
            flops=24 * blocks * rows * cols * width,
            bytes_accessed=2 * blocks * rows * cols,
            transcendentals=0,
        ),
    )(tile_mask, piece, ratings, item_factors)


def variation_kernel(group, near_ref, weight_ref, target_ref, dual_ref, out_ref, extra_ref, div_ref):
    blocks, degree = dual_ref.shape[:2]

    for sweep in range(ITERS):
        source = target_ref if sweep == 0 else extra_ref
        div_ref[...] = jnp.zeros_like(div_ref)

        def edges(step, _):
            first = step * group
            todo = []
            for j in range(group):
                a = first + j
                here = source[a]
                total = None
                for k in range(degree):
                    e = a * degree + k
                    to = near_ref[e]
                    w = weight_ref[e]
                    flux = dual_ref[a, k] if sweep == 0 else out_ref[a, k]
                    moved = flux + dual_step * (here - source[to])
                    square = jnp.sum(moved * moved, axis=-1, keepdims=True)
                    flux = moved * (w * lax.rsqrt(jnp.maximum(square, w * w)))
                    out_ref[a, k] = flux
                    total = flux if total is None else total + flux
                    todo.append((to, -flux))
                todo.append((a, total))
            for place, term in todo:
                div_ref[place] += term
            return 0

        lax.fori_loop(0, blocks // group, edges, 0)

        target = target_ref[...]
        primal = target if sweep == 0 else out_ref[:, degree]
        newer = (primal - primal_step * div_ref[...] + primal_step * target) / (1.0 + primal_step)
        if sweep < ITERS - 1:
            extra_ref[...] = 2.0 * newer - primal
        out_ref[:, degree] = newer


def variation(near, weight, target, dual):
    blocks, degree, rows, width = dual.shape
    group = next(g for g in (4, 2, 1) if blocks % g == 0)
    vmem = pl.BlockSpec(memory_space=pltpu.VMEM)
    smem = pl.BlockSpec(memory_space=pltpu.SMEM)
    return pl.pallas_call(
        functools.partial(variation_kernel, group),
        out_shape=jax.ShapeDtypeStruct((blocks, degree + 1, rows, width), jnp.float32),
        in_specs=[smem, smem, vmem, vmem],
        out_specs=vmem,
        scratch_shapes=[
            pltpu.VMEM((blocks, rows, width), jnp.float32),
            pltpu.VMEM((blocks, rows, width), jnp.float32),
        ],
        compiler_params=pltpu.CompilerParams(vmem_limit_bytes=32 << 20),
        cost_estimate=pl.CostEstimate(
            flops=20 * ITERS * dual.size, bytes_accessed=8 * dual.size, transcendentals=0
        ),
    )(near.reshape(-1), weight.reshape(-1), target, dual)


def shards(ratings, tile_mask, user_factors, item_factors, neighbours, edge_weight, dual):
    blocks_here, sub_rows, width = user_factors.shape
    degree = neighbours.shape[1]
    user_count = lax.axis_size("user")
    item_count = lax.axis_size("item")
    item_cols = item_factors.shape[0]
    thin = sub_rows // user_count
    total_blocks = blocks_here * user_count

    def exchange(parts, axis):
        return lax.all_to_all(parts.astype(WIRE), axis, 0, 0, tiled=True).astype(jnp.float32)

    total_users = blocks_here * sub_rows * item_count * user_count
    total_items = item_cols * item_count
    user_scale = 1.0 / math.sqrt(total_items)
    item_scale = 1.0 / math.sqrt(total_users)

    dual_parts = dual.reshape(blocks_here, degree, user_count, thin, width).transpose(2, 0, 1, 3, 4)
    dual_rows = exchange(dual_parts, "user").reshape(total_blocks, degree, thin, width)

    piece = lax.all_gather(user_factors, "item", axis=1, tiled=True)
    user_term, item_term = gradients(tile_mask, piece, ratings, item_factors, item_count)
    user_term, item_term, dual_rows = lax.optimization_barrier((user_term, item_term, dual_rows))

    user_grad = jnp.sum(exchange(user_term * user_scale, "item"), axis=0)
    item_parts = (item_term * item_scale).reshape(user_count, item_cols // user_count, width)
    item_parts = exchange(item_parts, "user")
    user_grad, item_parts = lax.optimization_barrier((user_grad, item_parts))
    item_own = jnp.sum(item_parts, axis=0)
    target = user_factors.astype(jnp.float32) - descent * user_grad
    target_parts = target.reshape(blocks_here, user_count, thin, width).transpose(1, 0, 2, 3)
    item_grad = lax.all_gather(item_own, "user", axis=0, tiled=True)
    target_rows = exchange(target_parts, "user").reshape(total_blocks, thin, width)
    result = variation(neighbours, edge_weight, target_rows, dual_rows)
    result, item_grad = lax.optimization_barrier((result, item_grad))
    result = result.reshape(user_count, blocks_here, degree + 1, thin, width)
    result = exchange(result, "user")
    result = result.transpose(1, 2, 0, 3, 4).reshape(blocks_here, degree + 1, sub_rows, width)
    return (result[:, degree], result[:, :degree], item_grad)


def solution(mesh):
    in_specs = (
        P("user", "item"),
        P("user", "item"),
        P("user", "item", None),
        P("item", None),
        P(),
        P(),
        P("user", None, "item", None),
    )
    out_specs = (P("user", "item", None), P("user", None, "item", None), P("item", None))
    return jax.shard_map(shards, mesh=mesh, in_specs=in_specs, out_specs=out_specs, check_vma=False)
```

```python
import functools
import math

import jax
import jax.numpy as jnp
from jax import lax
from jax.experimental import pallas as pl
from jax.experimental.pallas import tpu as pltpu
from jax.sharding import PartitionSpec as P

ITERS = 2
WIRE = jnp.float16

descent = 0.5
dual_step = 0.5
primal_step = 0.25


def gradient_kernel(seen_ref, piece_ref, rating_ref, item_ref, user_out, item_out, total):
    b = pl.program_id(0)
    parts, _, sub, _ = user_out.shape

    @pl.when(b == 0)
    def _():
        total[...] = jnp.zeros_like(total)

    users = piece_ref[0]
    items = item_ref[...]
    scores = lax.dot_general(
        users, items, (((1,), (1,)), ((), ())), preferred_element_type=jnp.float32
    )
    errors = (seen_ref[0] * (scores - rating_ref[...].astype(jnp.float32))).astype(jnp.bfloat16)
    term = jnp.dot(errors, items, preferred_element_type=jnp.float32)
    for p in range(parts):
        user_out[p, 0] = term[p * sub : (p + 1) * sub]
    total[...] += jnp.dot(users.T, errors, preferred_element_type=jnp.float32)

    @pl.when(b == pl.num_programs(0) - 1)
    def _():
        item_out[...] = total[...].T


def gradients(tile_mask, piece, ratings, item_factors, parts):
    blocks, rows, width = piece.shape
    cols = item_factors.shape[0]
    sub = rows // parts
    seen = jnp.repeat(tile_mask.astype(jnp.float32), cols // tile_mask.shape[1], axis=1)
    return pl.pallas_call(
        gradient_kernel,
        out_shape=(
            jax.ShapeDtypeStruct((parts, blocks, sub, width), jnp.float32),
            jax.ShapeDtypeStruct((cols, width), jnp.float32),
        ),
        grid=(blocks,),
        in_specs=[
            pl.BlockSpec((1, 1, cols), lambda b: (b, 0, 0)),
            pl.BlockSpec((1, rows, width), lambda b: (b, 0, 0)),
            pl.BlockSpec((rows, cols), lambda b: (b, 0)),
            pl.BlockSpec((cols, width), lambda b: (0, 0)),
        ],
        out_specs=[
            pl.BlockSpec((parts, 1, sub, width), lambda b: (0, b, 0, 0)),
            pl.BlockSpec((cols, width), lambda b: (0, 0)),
        ],
        scratch_shapes=[pltpu.VMEM((width, cols), jnp.float32)],
        compiler_params=pltpu.CompilerParams(vmem_limit_bytes=52 << 20),
        cost_estimate=pl.CostEstimate(
            flops=24 * blocks * rows * cols * width,
            bytes_accessed=2 * blocks * rows * cols,
            transcendentals=0,
        ),
    )(seen[:, None, :], piece, ratings, item_factors)


def variation_kernel(group, near_ref, weight_ref, target_ref, dual_ref, out_ref, extra_ref, div_ref):
    blocks, degree = dual_ref.shape[:2]

    for sweep in range(ITERS):
        source = target_ref if sweep == 0 else extra_ref
        div_ref[...] = jnp.zeros_like(div_ref)

        def edges(step, _):
            first = step * group
            todo = []
            for j in range(group):
                a = first + j
                here = source[a]
                total = None
                for k in range(degree):
                    e = a * degree + k
                    to = near_ref[e]
                    w = weight_ref[e]
                    flux = dual_ref[a, k] if sweep == 0 else out_ref[a, k]
                    moved = flux + dual_step * (here - source[to])
                    square = jnp.sum(moved * moved, axis=-1, keepdims=True)
                    flux = moved * (w * lax.rsqrt(jnp.maximum(square, w * w)))
                    out_ref[a, k] = flux
                    total = flux if total is None else total + flux
                    todo.append((to, -flux))
                todo.append((a, total))
            for place, term in todo:
                div_ref[place] += term
            return 0

        lax.fori_loop(0, blocks // group, edges, 0)

        target = target_ref[...]
        primal = target if sweep == 0 else out_ref[:, degree]
        newer = (primal - primal_step * div_ref[...] + primal_step * target) / (1.0 + primal_step)
        if sweep < ITERS - 1:
            extra_ref[...] = 2.0 * newer - primal
        out_ref[:, degree] = newer


def variation(near, weight, target, dual):
    blocks, degree, rows, width = dual.shape
    group = next(g for g in (4, 2, 1) if blocks % g == 0)
    vmem = pl.BlockSpec(memory_space=pltpu.VMEM)
    smem = pl.BlockSpec(memory_space=pltpu.SMEM)
    return pl.pallas_call(
        functools.partial(variation_kernel, group),
        out_shape=jax.ShapeDtypeStruct((blocks, degree + 1, rows, width), jnp.float32),
        in_specs=[smem, smem, vmem, vmem],
        out_specs=vmem,
        scratch_shapes=[
            pltpu.VMEM((blocks, rows, width), jnp.float32),
            pltpu.VMEM((blocks, rows, width), jnp.float32),
        ],
        compiler_params=pltpu.CompilerParams(vmem_limit_bytes=32 << 20),
        cost_estimate=pl.CostEstimate(
            flops=20 * ITERS * dual.size, bytes_accessed=8 * dual.size, transcendentals=0
        ),
    )(near.reshape(-1), weight.reshape(-1), target, dual)


def shards(ratings, tile_mask, user_factors, item_factors, neighbours, edge_weight, dual):
    blocks_here, sub_rows, width = user_factors.shape
    degree = neighbours.shape[1]
    user_count = lax.axis_size("user")
    item_count = lax.axis_size("item")
    item_cols = item_factors.shape[0]
    thin = sub_rows // user_count
    total_blocks = blocks_here * user_count

    def exchange(parts, axis):
        return lax.all_to_all(parts.astype(WIRE), axis, 0, 0, tiled=True).astype(jnp.float32)

    total_users = blocks_here * sub_rows * item_count * user_count
    total_items = item_cols * item_count
    user_scale = 1.0 / math.sqrt(total_items)
    item_scale = 1.0 / math.sqrt(total_users)

    dual_parts = dual.reshape(blocks_here, degree, user_count, thin, width).transpose(2, 0, 1, 3, 4)
    dual_rows = exchange(dual_parts, "user").reshape(total_blocks, degree, thin, width)

    piece = lax.all_gather(user_factors, "item", axis=1, tiled=True)
    user_term, item_term = gradients(tile_mask, piece, ratings, item_factors, item_count)
    user_term, item_term, dual_rows = lax.optimization_barrier((user_term, item_term, dual_rows))

    user_grad = jnp.sum(exchange(user_term * user_scale, "item"), axis=0)
    item_own = lax.psum_scatter(item_term, "user", scatter_dimension=0, tiled=True)
    user_grad, item_own = lax.optimization_barrier((user_grad, item_own))
    item_own = (item_own * (item_scale / user_count)).astype(WIRE)
    target = user_factors.astype(jnp.float32) - descent * user_grad
    target_parts = target.reshape(blocks_here, user_count, thin, width).transpose(1, 0, 2, 3)
    item_grad = lax.all_gather(item_own, "user", axis=0, tiled=True)
    target_rows = exchange(target_parts, "user").reshape(total_blocks, thin, width)
    result = variation(neighbours, edge_weight, target_rows, dual_rows)
    result, item_grad = lax.optimization_barrier((result, item_grad))
    item_grad = item_grad.astype(jnp.float32) * user_count
    result = result.reshape(user_count, blocks_here, degree + 1, thin, width)
    result = exchange(result, "user")
    result = result.transpose(1, 2, 0, 3, 4).reshape(blocks_here, degree + 1, sub_rows, width)
    return (result[:, degree], result[:, :degree], item_grad)


def solution(mesh):
    in_specs = (
        P("user", "item"),
        P("user", "item"),
        P("user", "item", None),
        P("item", None),
        P(),
        P(),
        P("user", None, "item", None),
    )
    out_specs = (P("user", "item", None), P("user", None, "item", None), P("item", None))
    return jax.shard_map(shards, mesh=mesh, in_specs=in_specs, out_specs=out_specs, check_vma=False)
```

```python
import functools
import math

import jax
import jax.numpy as jnp
from jax import lax
from jax.experimental import pallas as pl
from jax.experimental.pallas import tpu as pltpu
from jax.sharding import PartitionSpec as P

ITERS = 2
WIRE = jnp.float16

descent = 0.5
dual_step = 0.5
primal_step = 0.25


def gradient_kernel(seen_ref, piece_ref, rating_ref, item_ref, user_out, item_out, total):
    b = pl.program_id(0)
    parts, _, sub, _ = user_out.shape

    @pl.when(b == 0)
    def _():
        total[...] = jnp.zeros_like(total)

    users = piece_ref[0]
    items = item_ref[...]
    scores = lax.dot_general(
        users, items, (((1,), (1,)), ((), ())), preferred_element_type=jnp.float32
    )
    errors = (seen_ref[0] * (scores - rating_ref[...].astype(jnp.float32))).astype(jnp.bfloat16)
    term = jnp.dot(errors, items, preferred_element_type=jnp.float32)
    for p in range(parts):
        user_out[p, 0] = term[p * sub : (p + 1) * sub]
    total[...] += jnp.dot(users.T, errors, preferred_element_type=jnp.float32)

    @pl.when(b == pl.num_programs(0) - 1)
    def _():
        item_out[...] = total[...].T


def gradients(tile_mask, piece, ratings, item_factors, parts):
    blocks, rows, width = piece.shape
    cols = item_factors.shape[0]
    sub = rows // parts
    seen = jnp.repeat(tile_mask.astype(jnp.float32), cols // tile_mask.shape[1], axis=1)
    return pl.pallas_call(
        gradient_kernel,
        out_shape=(
            jax.ShapeDtypeStruct((parts, blocks, sub, width), jnp.float32),
            jax.ShapeDtypeStruct((cols, width), jnp.float32),
        ),
        grid=(blocks,),
        in_specs=[
            pl.BlockSpec((1, 1, cols), lambda b: (b, 0, 0)),
            pl.BlockSpec((1, rows, width), lambda b: (b, 0, 0)),
            pl.BlockSpec((rows, cols), lambda b: (b, 0)),
            pl.BlockSpec((cols, width), lambda b: (0, 0)),
        ],
        out_specs=[
            pl.BlockSpec((parts, 1, sub, width), lambda b: (0, b, 0, 0)),
            pl.BlockSpec((cols, width), lambda b: (0, 0)),
        ],
        scratch_shapes=[pltpu.VMEM((width, cols), jnp.float32)],
        compiler_params=pltpu.CompilerParams(vmem_limit_bytes=52 << 20),
        cost_estimate=pl.CostEstimate(
            flops=24 * blocks * rows * cols * width,
            bytes_accessed=2 * blocks * rows * cols,
            transcendentals=0,
        ),
    )(seen[:, None, :], piece, ratings, item_factors)


def variation_kernel(group, near_ref, weight_ref, target_ref, dual_ref, out_ref, extra_ref, div_ref):
    blocks, degree = dual_ref.shape[:2]

    for sweep in range(ITERS):
        source = target_ref if sweep == 0 else extra_ref
        div_ref[...] = jnp.zeros_like(div_ref)

        def edges(step, _):
            first = step * group
            todo = []
            for j in range(group):
                a = first + j
                here = source[a]
                total = None
                for k in range(degree):
                    e = a * degree + k
                    to = near_ref[e]
                    w = weight_ref[e]
                    flux = dual_ref[a, k] if sweep == 0 else out_ref[a, k]
                    moved = flux + dual_step * (here - source[to])
                    square = jnp.sum(moved * moved, axis=-1, keepdims=True)
                    flux = moved * (w * lax.rsqrt(jnp.maximum(square, w * w)))
                    out_ref[a, k] = flux
                    total = flux if total is None else total + flux
                    todo.append((to, -flux))
                todo.append((a, total))
            for place, term in todo:
                div_ref[place] += term
            return 0

        lax.fori_loop(0, blocks // group, edges, 0)

        target = target_ref[...]
        primal = target if sweep == 0 else out_ref[:, degree]
        newer = (primal - primal_step * div_ref[...] + primal_step * target) / (1.0 + primal_step)
        if sweep < ITERS - 1:
            extra_ref[...] = 2.0 * newer - primal
        out_ref[:, degree] = newer


def variation(near, weight, target, dual):
    blocks, degree, rows, width = dual.shape
    group = next(g for g in (4, 2, 1) if blocks % g == 0)
    vmem = pl.BlockSpec(memory_space=pltpu.VMEM)
    smem = pl.BlockSpec(memory_space=pltpu.SMEM)
    return pl.pallas_call(
        functools.partial(variation_kernel, group),
        out_shape=jax.ShapeDtypeStruct((blocks, degree + 1, rows, width), jnp.float32),
        in_specs=[smem, smem, vmem, vmem],
        out_specs=vmem,
        scratch_shapes=[
            pltpu.VMEM((blocks, rows, width), jnp.float32),
            pltpu.VMEM((blocks, rows, width), jnp.float32),
        ],
        compiler_params=pltpu.CompilerParams(vmem_limit_bytes=32 << 20),
        cost_estimate=pl.CostEstimate(
            flops=20 * ITERS * dual.size, bytes_accessed=8 * dual.size, transcendentals=0
        ),
    )(near.reshape(-1), weight.reshape(-1), target, dual)


def shards(ratings, tile_mask, user_factors, item_factors, neighbours, edge_weight, dual):
    blocks_here, sub_rows, width = user_factors.shape
    degree = neighbours.shape[1]
    user_count = lax.axis_size("user")
    item_count = lax.axis_size("item")
    item_cols = item_factors.shape[0]
    thin = sub_rows // user_count
    total_blocks = blocks_here * user_count

    def exchange(parts, axis):
        return lax.all_to_all(parts.astype(WIRE), axis, 0, 0, tiled=True).astype(jnp.float32)

    total_users = blocks_here * sub_rows * item_count * user_count
    total_items = item_cols * item_count
    user_scale = 1.0 / math.sqrt(total_items)
    item_scale = 1.0 / math.sqrt(total_users)

    dual_parts = dual.reshape(blocks_here, degree, user_count, thin, width).transpose(2, 0, 1, 3, 4)
    dual_rows = exchange(dual_parts, "user").reshape(total_blocks, degree, thin, width)

    piece = lax.all_gather(user_factors, "item", axis=1, tiled=True)
    user_term, item_term = gradients(tile_mask, piece, ratings, item_factors, item_count)
    user_term, item_term, dual_rows = lax.optimization_barrier((user_term, item_term, dual_rows))

    user_grad = jnp.sum(exchange(user_term * user_scale, "item"), axis=0)
    item_parts = (item_term * item_scale).reshape(user_count, item_cols // user_count, width)
    item_parts = exchange(item_parts, "user")
    user_grad, item_parts = lax.optimization_barrier((user_grad, item_parts))
    item_own = jnp.sum(item_parts, axis=0)
    target = user_factors.astype(jnp.float32) - descent * user_grad
    target_parts = target.reshape(blocks_here, user_count, thin, width).transpose(1, 0, 2, 3)
    item_grad = lax.all_gather(item_own, "user", axis=0, tiled=True)
    target_rows = exchange(target_parts, "user").reshape(total_blocks, thin, width)
    result = variation(neighbours, edge_weight, target_rows, dual_rows)
    result, item_grad = lax.optimization_barrier((result, item_grad))
    result = result.reshape(user_count, blocks_here, degree + 1, thin, width)
    result = exchange(result, "user")
    result = result.transpose(1, 2, 0, 3, 4).reshape(blocks_here, degree + 1, sub_rows, width)
    return (result[:, degree], result[:, :degree], item_grad)


def solution(mesh):
    in_specs = (
        P("user", "item"),
        P("user", "item"),
        P("user", "item", None),
        P("item", None),
        P(),
        P(),
        P("user", None, "item", None),
    )
    out_specs = (P("user", "item", None), P("user", None, "item", None), P("item", None))
    return jax.shard_map(shards, mesh=mesh, in_specs=in_specs, out_specs=out_specs, check_vma=False)
```
